128 devices in a mesh: grp: 4 (over x_lo, core), chain: 32 (over z, x_hi, y).
Axes of the slice: x: 4 (x_hi: 2, x_lo: 2; x = x_hi * 2 + x_lo), y: 4, z: 4, core: 2. Of those that a mesh axis runs over, the one named last changes fastest.
Arguments:
- chain_rhs: bfloat16 [4, 512, 256, 256], P('grp', 'chain'), may hold values from -0.5 to 0.5
- diag_inverse: bfloat16 [4, 512, 256, 256], P('grp', 'chain'), may hold values from -1 to 1, as said below
- sub_blocks: bfloat16 [4, 512, 256, 256], P('grp', 'chain'), may hold values from -1 to 1
- root_blocks: bfloat16 [4, 1024, 256, 256], P('grp', 'chain'), may hold values from -0.03125 to 0.03125
- coupling_column: int32 [4, 1024], P('grp', 'chain'), may hold values from 0 to 15
- coupling_target: int32 [4, 1024], P('grp', 'chain'), may hold values from 0 to 31
- root_rhs: bfloat16 [32, 256, 256], P('chain'), may hold values from -6 to 6
- root_inverse: bfloat16 [32, 256, 256], P('chain'), may hold values from -1 to 1, as said below
Outputs:
- chain_solution: float32 [4, 512, 256, 256], P('grp', 'chain')
- root_solution: float32 [32, 256, 256], P('chain')
The draws below stay inside these ranges and needn't reach their ends.
Inputs may be any that keep to these rules, and one draw needn't show every extreme that they name: `diag_inverse`: unit lower triangular: ones on the diagonal and zeros above it. `root_inverse`: unit lower triangular: ones on the diagonal and zeros above it.
All inputs are finite; a program needn't handle non-finite values.
Results may differ from the reference program's by a relative error of at most 0.0003.
Values sent between devices are 32-bit elements; how exact they have to be, the bound alone decides.
No kernel may reach another device: no remote copies, remote signals or barrier semaphores. Data moves between devices by JAX's collectives and lax.ppermute only.
A program may use at most 128 MiB of HBM per device.

```python
import math
import jax
import jax.numpy as jnp
from jax import lax

NS = 256
NRHS = 256
KS = 16
NT = 32
CHAIN_BLOCKS = 512
COUPLINGS = 1024
ROOTS = 32
N_GRP = 4


def unit_lower(key, array_shape):
    block_order = array_shape[-1]
    entries = jnp.clip(jax.random.normal(key, array_shape, jnp.float32), -4.0, 4.0)
    spread = 0.5 * (2.0 / block_order) ** 0.5
    strict_lower = jnp.tril(jnp.ones((block_order, block_order), jnp.float32), -1)
    result = jnp.eye(block_order, dtype=jnp.float32) + entries * spread * strict_lower
    return result.astype(jnp.bfloat16)


def draw_diag_inverse(key, part):
    return unit_lower(jax.random.fold_in(key, 11), (N_GRP, CHAIN_BLOCKS, NS, NS))


def draw_root_inverse(key, part):
    return unit_lower(jax.random.fold_in(key, 23), (ROOTS, NS, NS))


def draw_sub_blocks(key, part):
    block_order = NS
    trace_value = block_order + 0.25 * (block_order - 1)
    decay_rate = -1.5 / CHAIN_BLOCKS
    correction = 1.39 / block_order
    spread = (math.exp(2.0 * decay_rate + correction) / trace_value) ** 0.5
    array_shape = (N_GRP, CHAIN_BLOCKS, NS, NS)
    subkey = jax.random.fold_in(key, 37)
    entries = jnp.clip(jax.random.normal(subkey, array_shape, jnp.float32), -4.0, 4.0)
    return (entries * spread).astype(jnp.bfloat16)


def set_ends(values, key, least, top_value):
    shape = values.shape
    spot = [jax.random.randint(jax.random.fold_in(key, axis), (), 0, shape[axis]) for axis in range(len(shape))]
    values = values.at[tuple(spot)].set(least)
    longest = shape.index(max(shape))
    spot[longest] = (spot[longest] + 1) % shape[longest]
    return values.at[tuple(spot)].set(top_value)


def block_levels(own_key, extent, shards, least, high):
    factor_of, own = 1.0, jax.random.fold_in(own_key, 6)
    for position, blocks in shards:
        draws = jnp.exp(jax.random.uniform(jax.random.fold_in(own, position), (blocks,), jnp.float32, least / len(shards), high / len(shards)))
        factor_of = factor_of * jnp.repeat(draws, extent[position] // blocks).reshape([-1 if axis == position else 1 for axis in range(len(extent))])
    return factor_of


def noise(key, extent, scale, reach, cuts=(), kind=jnp.bfloat16):
    values = jax.random.normal(key, extent, jnp.float32) * scale
    if len(cuts) > 0:
        values = block_levels(key, extent, cuts, -0.22, 0.18) * values
    return jnp.clip(values, min=-reach, max=reach).astype(kind)


def setup_inputs(seed: int = 0) -> dict:
    streams_of = jax.random.split(jax.random.key(seed), 9)
    chain_rhs = noise(streams_of[0], (N_GRP, CHAIN_BLOCKS, NS, NRHS), 0.08, 0.5, ((0, 4), (1, 32)))
    diag_inverse = draw_diag_inverse(jax.random.fold_in(streams_of[8], 71), 0)
    sub_blocks = draw_sub_blocks(jax.random.fold_in(streams_of[8], 71), 0)
    root_blocks = noise(streams_of[3], (N_GRP, COUPLINGS, NS, NS), (NS * N_GRP * NT) ** -0.5, 0.03125, ((0, 4), (1, 32)))
    coupling_column = set_ends(jax.random.randint(streams_of[4], (N_GRP, COUPLINGS), 0, KS), jax.random.fold_in(streams_of[4], 1), 0, KS - 1).astype(jnp.int32)
    coupling_target = set_ends(jax.random.randint(streams_of[5], (N_GRP, COUPLINGS), 0, ROOTS), jax.random.fold_in(streams_of[5], 1), 0, ROOTS - 1).astype(jnp.int32)
    root_rhs = noise(streams_of[6], (ROOTS, NS, NRHS), 1.0, 6.0, ((0, 32),))
    root_inverse = draw_root_inverse(jax.random.fold_in(streams_of[8], 71), 0)
    return dict(chain_rhs=chain_rhs, diag_inverse=diag_inverse, sub_blocks=sub_blocks, root_blocks=root_blocks, coupling_column=coupling_column, coupling_target=coupling_target, root_rhs=root_rhs, root_inverse=root_inverse)


HIGHEST = lax.Precision.HIGHEST


def sweep_blocks(previous, inverse, lower_blocks, right_side):
    def advance(carry, operands):
        inverse_block, lower_block, right_block = operands
        update = right_block.astype(jnp.float32) - jnp.dot(lower_block.astype(jnp.float32), carry, precision=HIGHEST, preferred_element_type=jnp.float32)
        solved = jnp.dot(inverse_block.astype(jnp.float32), update, precision=HIGHEST, preferred_element_type=jnp.float32)
        return solved, solved
    return lax.scan(advance, previous, (inverse, lower_blocks, right_side))


def reference(chain_rhs, diag_inverse, sub_blocks, root_blocks, coupling_column, coupling_target, root_rhs, root_inverse):
    zero_start = jnp.zeros((NS, NRHS), jnp.float32)

    def solve_group(operands):
        inverse, lower_blocks, right_side = operands
        return sweep_blocks(zero_start, inverse, lower_blocks, right_side)[1]

    chain_solution = lax.map(solve_group, (diag_inverse, sub_blocks, chain_rhs))
    block_index = ((jnp.arange(COUPLINGS, dtype=jnp.int32) // NT) * KS)[None, :] + coupling_column.astype(jnp.int32)
    group_index = jnp.broadcast_to(jnp.arange(N_GRP, dtype=jnp.int32)[:, None], (N_GRP, COUPLINGS))

    def flatten(array):
        return array.reshape((N_GRP * COUPLINGS,) + array.shape[2:])

    def add_coupling(partial_value, operands):
        block, group_at, column_at, target_at = operands
        term = jnp.dot(block.astype(jnp.float32), chain_solution[group_at, column_at], precision=HIGHEST, preferred_element_type=jnp.float32)
        return partial_value.at[target_at].add(term), None

    partial_value, _ = lax.scan(add_coupling, jnp.zeros((ROOTS, NS, NRHS), jnp.float32),
                          (flatten(root_blocks), flatten(group_index), flatten(block_index), flatten(coupling_target.astype(jnp.int32))))
    root_update = root_rhs.astype(jnp.float32) - partial_value
    root_solution = jnp.einsum("rij,rjn->rin", root_inverse.astype(jnp.float32), root_update, precision=HIGHEST)
    return chain_solution, root_solution
```

```python
import jax
import jax.numpy as jnp
from jax import lax
from jax.experimental import pallas as pl
from jax.experimental.pallas import tpu as pltpu
from jax.sharding import PartitionSpec as P

HIGHEST = lax.Precision.HIGHEST
F32, BF16 = jnp.float32, jnp.bfloat16

B = 256
KS = 16
NT = 32
ROOTS = 32
Q = 64
LIMIT = 16.0
LARGE = 1e30
AXES = ("grp", "chain")


def flat(x_lo, core, z, x_hi, y):
    return (x_lo * 2 + core) * 32 + z * 8 + x_hi * 4 + y


EVERY = [
    (x_lo, core, z, x_hi, y)
    for x_lo in range(2)
    for core in range(2)
    for z in range(4)
    for x_hi in range(2)
    for y in range(4)
]


def permute(value, target):
    pairs = []
    for place in EVERY:
        to = target(*place)
        if to is not None:
            pairs.append((flat(*place), flat(*to)))
    return lax.ppermute(value, AXES, pairs)


def split(value):
    high = value.astype(BF16)
    return high, (value - high.astype(F32)).astype(BF16)


def dot(a, b):
    return jnp.dot(a, b, preferred_element_type=F32)


def dot3(ah, al, bh, bl):
    return dot(
        jnp.concatenate([ah, al, ah], axis=1), jnp.concatenate([bh, bh, bl], axis=0)
    )


def product(a, b):
    return dot3(*split(a), *split(b))


def beyond(value, limit):
    rows = value.shape[0] // 8
    over = jnp.where(jnp.abs(value) <= limit, 0.0, 1.0)
    return jnp.max(over.reshape(rows, 8, value.shape[1]), axis=0)


def local_kernel(
    pos, d_ref, s_ref, b_ref, ph_ref, pl_ref, c_ref, g0, g1, g2, g3, bad_ref,
    ath, atl, ct, th, tl,
):
    t = pl.program_id(0)

    @pl.when(t == 0)
    def _():
        row = lax.broadcasted_iota(jnp.int32, (B, B), 0)
        col = lax.broadcasted_iota(jnp.int32, (B, B), 1)
        eye = jnp.where(row == col, 1.0, 0.0).astype(BF16)
        ath[1] = eye
        atl[1] = jnp.zeros((B, B), BF16)
        ct[1] = jnp.zeros((B, B), F32)
        th[:B] = eye
        th[B:] = jnp.zeros((B, B), BF16)
        tl[...] = jnp.zeros_like(tl)
        bad_ref[...] = jnp.zeros_like(bad_ref)

    old, now = lax.rem(t + 1, 2), lax.rem(t, 2)
    fresh = dot3(th[...], tl[...], ath[old], atl[old])
    moved, part = fresh[:B], fresh[B:] + ct[old]
    mh, ml = split(moved)
    xh, xl = split(part)
    th[:B], tl[:B] = mh, ml
    th[B:], tl[B:] = xh, xl
    ph_ref[0], pl_ref[0] = mh, ml
    c_ref[0] = part
    bad_ref[...] = jnp.maximum(bad_ref[...], beyond(moved, LIMIT))

    turned = (((0,), (1,)), ((), ()))
    at = -lax.dot_general(s_ref[0, 0], d_ref[0, 0], turned, preferred_element_type=F32)
    ah, al = split(at)
    ath[now] = ah
    atl[now] = al
    ct[now] = lax.dot_general(b_ref[0, 0], d_ref[0, 0], turned, preferred_element_type=F32)

    @pl.when(t == KS)
    def _():
        for step, g in enumerate((g0, g1, g2, g3)):
            g[:B] = moved
            start = pl.multiple_of(lax.rem(pos[0] + step, 4) * Q, Q)
            g[B:] = c_ref[0, pl.ds(start, Q), :]


def local_scan(pos, inverse, lower, right):
    def block(t, pos):
        return (0, jnp.minimum(t, KS - 1), 0, 0)

    def out(t, pos):
        return (jnp.maximum(t - 1, 0), 0, 0)

    def whole(t, pos):
        return (0, 0)

    piece = jax.ShapeDtypeStruct((B + Q, B), F32)
    return pl.pallas_call(
        local_kernel,
        grid_spec=pltpu.PrefetchScalarGridSpec(
            num_scalar_prefetch=1,
            grid=(KS + 1,),
            in_specs=[pl.BlockSpec((1, 1, B, B), block)] * 3,
            out_specs=[pl.BlockSpec((1, B, B), out)] * 3
            + [pl.BlockSpec((B + Q, B), whole)] * 4
            + [pl.BlockSpec((8, B), whole)],
            scratch_shapes=[
                pltpu.VMEM((2, B, B), BF16),
                pltpu.VMEM((2, B, B), BF16),
                pltpu.VMEM((2, B, B), F32),
                pltpu.VMEM((2 * B, B), BF16),
                pltpu.VMEM((2 * B, B), BF16),
            ],
        ),
        out_shape=[
            jax.ShapeDtypeStruct((KS, B, B), BF16),
            jax.ShapeDtypeStruct((KS, B, B), BF16),
            jax.ShapeDtypeStruct((KS, B, B), F32),
            piece, piece, piece, piece,
            jax.ShapeDtypeStruct((8, B), F32),
        ],
        name="local_scan",
    )(pos, inverse, lower, right)


def group_kernel(pos, g0, g1, g2, g3, w_ref, wg_ref, bad_ref, buf, sem):
    copies = []
    for step, g in enumerate((g0, g1, g2, g3)):
        place = lax.rem(pos[0] + 4 - step, 4)
        copies.append(pltpu.make_async_copy(g, buf.at[place], sem.at[step]))
    for copy in copies:
        copy.start()
    for copy in copies:
        copy.wait()
    w = buf[0]
    w_ref[0] = w
    bad = jnp.zeros((8, B), F32)
    for k in range(1, 4):
        w = product(w, buf[k, :B])
        w = jnp.concatenate([w[:B], w[B:] + buf[k, B:]], axis=0)
        bad = jnp.maximum(bad, beyond(w[:B], LIMIT))
        if k < 3:
            w_ref[k] = w
    wg_ref[...] = w
    bad_ref[...] = bad


SMEM = pl.BlockSpec(memory_space=pltpu.SMEM)
VMEM = pl.BlockSpec(memory_space=pltpu.VMEM)
ANY = pl.BlockSpec(memory_space=pl.ANY)


def group_scan(pos, pieces):
    return pl.pallas_call(
        group_kernel,
        in_specs=[SMEM] + [ANY] * 4,
        out_specs=[VMEM] * 3,
        out_shape=[
            jax.ShapeDtypeStruct((3, B + Q, B), F32),
            jax.ShapeDtypeStruct((B + Q, B), F32),
            jax.ShapeDtypeStruct((8, B), F32),
        ],
        scratch_shapes=[pltpu.VMEM((4, B + Q, B), F32), pltpu.SemaphoreType.DMA((4,))],
        name="group_scan",
    )(pos, *pieces)


def pair_kernel(own, other, mh_ref, ml_ref, c_ref, bad_ref):
    z = product(other[...], own[:B])
    bad_ref[...] = beyond(z[:B], LIMIT)
    mh_ref[...], ml_ref[...] = split(z[:B])
    c_ref[...] = z[B:] + own[B:]


def pair_scan(own, other):
    return pl.pallas_call(
        pair_kernel,
        in_specs=[VMEM] * 2,
        out_specs=[VMEM] * 4,
        out_shape=[
            jax.ShapeDtypeStruct((B, B), BF16),
            jax.ShapeDtypeStruct((B, B), BF16),
            jax.ShapeDtypeStruct((Q, B), F32),
            jax.ShapeDtypeStruct((8, B), F32),
        ],
        name="pair_scan",
    )(own, other)


def hop_kernel(x, mh, ml, c, out):
    out[...] = dot3(*split(x[...]), mh[...], ml[...]) + c[...]


def hop(x, mh, ml, c):
    return pl.pallas_call(
        hop_kernel,
        in_specs=[VMEM] * 4,
        out_specs=VMEM,
        out_shape=jax.ShapeDtypeStruct((Q, B), F32),
        name="hop",
    )(x, mh, ml, c)


def start_kernel(pos, z_in, x_in, other, w_ref, o0, o1, o2, o3, all_):
    through = product(z_in[...], other[:B]) + other[B:]
    begin = jnp.where(pos[1] == 1, through, x_in[...])
    all_[0] = begin
    bh, bl = split(begin)
    for k in range(3):
        all_[k + 1] = dot3(bh, bl, *split(w_ref[k, :B])) + w_ref[k, B:]
    for step, o in enumerate((o0, o1, o2, o3)):
        o[...] = all_[lax.rem(pos[0] + step, 4)]


def starts(pos, z_in, x_in, other, w):
    return pl.pallas_call(
        start_kernel,
        in_specs=[SMEM] + [VMEM] * 4,
        out_specs=[VMEM] * 4,
        out_shape=[jax.ShapeDtypeStruct((Q, B), F32)] * 4,
        scratch_shapes=[pltpu.VMEM((4, Q, B), F32)],
        name="starts",
    )(pos, z_in, x_in, other, w)


def couple(col, tgt, k, r, xh, xl, acc):
    c, t = col[k], tgt[k]
    acc[t] += dot(
        jnp.concatenate([r, r], axis=1), jnp.concatenate([xh[c], xl[c]], axis=0)
    )


def expand_kernel(
    pos, col, tgt, q0, q1, q2, q3, ph, pl_, c, bad1, bad2, bad3, r,
    sol, xh, xl, acc, xth, xtl, bad,
):
    t = pl.program_id(0)

    @pl.when(t == 0)
    def _():
        for step, q in enumerate((q0, q1, q2, q3)):
            start = pl.multiple_of(lax.rem(pos[0] + 4 - step, 4) * Q, Q)
            xth[pl.ds(start, Q), :], xtl[pl.ds(start, Q), :] = split(q[...])
        bad[...] = jnp.maximum(jnp.maximum(bad1[...], bad2[...]), bad3[...])

    @pl.when(t < KS)
    def _():
        xt = dot3(xth[...], xtl[...], ph[0], pl_[0]) + c[0]
        x = xt.T
        sol[0, 0] = x
        bad[...] = jnp.maximum(bad[...], beyond(x, LARGE))
        xh[t], xl[t] = split(x)

    @pl.when(t == KS)
    def _():
        poison = jnp.where(jnp.max(bad[...]) > 0.0, jnp.nan, 0.0)
        acc[...] = jnp.full(acc.shape, poison, F32)

    @pl.when(t >= KS)
    def _():
        start = pl.multiple_of((1 - pos[2]) * 128, 128)
        couple(col, tgt, t - KS, r[0, 0, pl.ds(start, 128), :], xh, xl, acc)


def expand(pos, col, tgt, quarters, ph, pl_, c, bads, root_blocks):
    def block(t, *_):
        return (jnp.minimum(t, KS - 1), 0, 0)

    def two(t, *_):
        return (0, 0)

    def three(t, *_):
        return (0, 0, 0)

    return pl.pallas_call(
        expand_kernel,
        grid_spec=pltpu.PrefetchScalarGridSpec(
            num_scalar_prefetch=3,
            grid=(KS + NT,),
            in_specs=[pl.BlockSpec((Q, B), two)] * 4
            + [pl.BlockSpec((1, B, B), block)] * 3
            + [pl.BlockSpec((8, B), two)] * 3
            + [pl.BlockSpec((1, 1, B, B), lambda t, *_: (0, jnp.maximum(t - KS, 0), 0, 0))],
            out_specs=[
                pl.BlockSpec((1, 1, B, B), lambda t, *_: (0, jnp.minimum(t, KS - 1), 0, 0)),
                pl.BlockSpec((KS, B, B), three),
                pl.BlockSpec((KS, B, B), three),
                pl.BlockSpec((ROOTS, 128, B), three),
            ],
            scratch_shapes=[
                pltpu.VMEM((B, B), BF16),
                pltpu.VMEM((B, B), BF16),
                pltpu.VMEM((8, B), F32),
            ],
        ),
        out_shape=[
            jax.ShapeDtypeStruct((1, KS, B, B), F32),
            jax.ShapeDtypeStruct((KS, B, B), BF16),
            jax.ShapeDtypeStruct((KS, B, B), BF16),
            jax.ShapeDtypeStruct((ROOTS, 128, B), F32),
        ],
        compiler_params=pltpu.CompilerParams(vmem_limit_bytes=60 << 20),
        cost_estimate=pl.CostEstimate(flops=10**10, bytes_accessed=30 << 20, transcendentals=0),
        name="expand",
    )(pos, col, tgt, *quarters, ph, pl_, c, *bads, root_blocks)


def keep_kernel(pos, col, tgt, xh, xl, r, acc):
    t = pl.program_id(0)

    @pl.when(t == 0)
    def _():
        acc[...] = jnp.zeros_like(acc)

    start = pl.multiple_of(pos[2] * 128, 128)
    couple(col, tgt, t, r[0, 0, pl.ds(start, 128), :], xh, xl, acc)


def keep_half(pos, col, tgt, xh, xl, root_blocks):
    def three(t, *_):
        return (0, 0, 0)

    return pl.pallas_call(
        keep_kernel,
        grid_spec=pltpu.PrefetchScalarGridSpec(
            num_scalar_prefetch=3,
            grid=(NT,),
            in_specs=[pl.BlockSpec((KS, B, B), three)] * 2
            + [pl.BlockSpec((1, 1, B, B), lambda t, *_: (0, t, 0, 0))],
            out_specs=pl.BlockSpec((ROOTS, 128, B), three),
        ),
        out_shape=jax.ShapeDtypeStruct((ROOTS, 128, B), F32),
        compiler_params=pltpu.CompilerParams(vmem_limit_bytes=60 << 20),
        cost_estimate=pl.CostEstimate(flops=5 * 10**9, bytes_accessed=16 << 20, transcendentals=0),
        name="keep_half",
    )(pos, col, tgt, xh, xl, root_blocks)


def root_kernel(rhs, inv, mine, theirs, pos, out, total):
    core = pos[2]
    total[pl.ds(pl.multiple_of(core * 128, 128), 128), :] = mine[...]
    total[pl.ds(pl.multiple_of((1 - core) * 128, 128), 128), :] = theirs[...]
    uh, ul = split(rhs[0].astype(F32) - total[...])
    i = inv[0]
    out[0] = dot(jnp.concatenate([i, i], axis=1), jnp.concatenate([uh, ul], axis=0))


def root_solve(pos, rhs, inv, mine, theirs):
    return pl.pallas_call(
        root_kernel,
        in_specs=[VMEM] * 4 + [SMEM],
        out_specs=VMEM,
        out_shape=jax.ShapeDtypeStruct((1, B, B), F32),
        scratch_shapes=[pltpu.VMEM((B, B), F32)],
        name="root_solve",
    )(rhs, inv, mine, theirs, pos)


def other_core(value):
    return permute(value, lambda l, c, z, h, y: (l, 1 - c, z, h, y))


def other_chip(value):
    return permute(value, lambda l, c, z, h, y: (1 - l, c, z, h, y))


def reduce_roots(sent, kept):
    both = kept + other_core(sent)
    pieces = lax.all_to_all(both, "chain", 0, 0, tiled=True)
    mine = jnp.sum(pieces, axis=0)
    mine = mine + other_chip(mine)
    return mine, other_core(mine)


def chain_fast(pos, inverse, lower, right):
    ph, pl_, c, *pieces, bad1 = local_scan(pos, inverse, lower, right)

    def along(step):
        return lambda l, k, z, h, y: (l, k, z, h, (y + step) % 4)

    pieces = [pieces[0]] + [permute(pieces[s], along(s)) for s in (1, 2, 3)]
    w, own, bad2 = group_scan(pos, pieces)
    other = permute(own, lambda l, k, z, h, y: (l, k, z, 1, y) if h == 0 else None)
    mh, ml, cz, bad3 = pair_scan(own, other)

    def up(l, k, z, h, y):
        return (l, k, z + 1, 1, y) if h == 1 and z < 3 else None

    def across(l, k, z, h, y):
        return (l, k, z + 1, 0, y) if h == 1 and z < 3 else None

    x = cz
    x = hop(permute(x, up), mh, ml, cz)
    x = hop(permute(x, up), mh, ml, cz)
    z_in, x_in = permute(x, up), permute(x, across)
    quarters = starts(pos, z_in, x_in, other, w)
    quarters = [quarters[0]] + [permute(quarters[s], along(s)) for s in (1, 2, 3)]
    return ph, pl_, c, quarters, (bad1, bad2, bad3)


def sweep_blocks(previous, inverse, lower_blocks, right_side):
    def advance(carry, operands):
        inverse_block, lower_block, right_block = operands
        update = right_block.astype(F32) - jnp.dot(
            lower_block.astype(F32), carry, precision=HIGHEST, preferred_element_type=F32
        )
        solved = jnp.dot(
            inverse_block.astype(F32), update, precision=HIGHEST, preferred_element_type=F32
        )
        return (solved, solved)

    return lax.scan(advance, previous, (inverse, lower_blocks, right_side))


def chain_slow(inverse, lower, right):
    inverse, lower, right = inverse[0], lower[0], right[0]
    position = lax.axis_index("chain")
    length = lax.axis_size("chain")

    def one_turn(turn, carry):
        incoming, solved = carry

        def work(operands):
            return sweep_blocks(operands[0], inverse, lower, right)

        outgoing, solved = lax.cond(turn == position, work, lambda o: o, (incoming, solved))
        incoming = permute(
            outgoing,
            lambda l, k, z, h, y: (
                (l, k, *_place(z * 8 + h * 4 + y + 1)) if z * 8 + h * 4 + y < 31 else None
            ),
        )
        return (incoming, solved)

    begin = (jnp.zeros((B, B), F32), jnp.zeros((KS, B, B), F32))
    return lax.fori_loop(0, length, one_turn, begin)[1]


def _place(index):
    return index // 8, index // 4 % 2, index % 4


def slow_partial(solved, columns, targets, root_blocks):
    def add(partial, operands):
        block, column, target = operands
        term = jnp.dot(
            block.astype(F32), solved[column], precision=HIGHEST, preferred_element_type=F32
        )
        return (partial.at[target].add(term), None)

    zero = jnp.zeros((ROOTS, B, B), F32)
    return lax.scan(add, zero, (root_blocks[0], columns, targets))[0]


def per_device(
    chain_rhs,
    diag_inverse,
    sub_blocks,
    root_blocks,
    coupling_column,
    coupling_target,
    root_rhs,
    root_inverse,
):
    place = lax.axis_index("chain")
    core = lax.axis_index("grp") % 2
    pos = jnp.stack([place % 4, place // 4 % 2, core]).astype(jnp.int32)
    col, tgt = coupling_column[0], coupling_target[0]

    ph, pl_, c, quarters, bads = chain_fast(pos, diag_inverse, sub_blocks, chain_rhs)
    solution_, xh, xl, sent = expand(
        pos, col, tgt, quarters, ph, pl_, c, bads, root_blocks
    )
    kept = keep_half(pos, col, tgt, xh, xl, root_blocks)
    mine, theirs = reduce_roots(sent, kept)
    root = root_solve(pos, root_rhs, root_inverse, mine, theirs)
    again = jnp.isnan(mine[0, 0]) | jnp.isnan(theirs[0, 0])

    def redo(state):
        solved = chain_slow(diag_inverse, sub_blocks, chain_rhs)
        partial = slow_partial(solved, col, tgt, root_blocks)
        halves = partial.reshape(ROOTS, 2, 128, B)
        kept = lax.dynamic_index_in_dim(halves, core, 1, False)
        sent = lax.dynamic_index_in_dim(halves, 1 - core, 1, False)
        mine, theirs = reduce_roots(sent, kept)
        root = root_solve(pos, root_rhs, root_inverse, mine, theirs)
        return (jnp.zeros((), jnp.bool_), solved[None], root)

    _, solution_, root = lax.while_loop(lambda s: s[0], redo, (again, solution_, root))
    return (solution_, root)


def solution(mesh):
    in_specs = (
        P("grp", "chain", None, None),
        P("grp", "chain", None, None),
        P("grp", "chain", None, None),
        P("grp", "chain", None, None),
        P("grp", "chain"),
        P("grp", "chain"),
        P("chain", None, None),
        P("chain", None, None),
    )
    out_specs = (P("grp", "chain", None, None), P("chain", None, None))
    return jax.shard_map(
        per_device, mesh=mesh, in_specs=in_specs, out_specs=out_specs, check_vma=False
    )
```

```python
import jax
import jax.numpy as jnp
from jax import lax
from jax.experimental import pallas as pl
from jax.experimental.pallas import tpu as pltpu
from jax.sharding import PartitionSpec as P

HIGHEST = lax.Precision.HIGHEST
F32, BF16 = jnp.float32, jnp.bfloat16

B = 256
KS = 16
NT = 32
ROOTS = 32
Q = 64
LIMIT = 16.0
LARGE = 1e30
AXES = ("grp", "chain")


def flat(x_lo, core, z, x_hi, y):
    return (x_lo * 2 + core) * 32 + z * 8 + x_hi * 4 + y


EVERY = [
    (x_lo, core, z, x_hi, y)
    for x_lo in range(2)
    for core in range(2)
    for z in range(4)
    for x_hi in range(2)
    for y in range(4)
]


def permute(value, target):
    pairs = []
    for place in EVERY:
        to = target(*place)
        if to is not None:
            pairs.append((flat(*place), flat(*to)))
    return lax.ppermute(value, AXES, pairs)


def split(value):
    high = value.astype(BF16)
    return high, (value - high.astype(F32)).astype(BF16)


def dot(a, b):
    return jnp.dot(a, b, preferred_element_type=F32)


def dot3(ah, al, bh, bl):
    return dot(
        jnp.concatenate([ah, al, ah], axis=1), jnp.concatenate([bh, bh, bl], axis=0)
    )


def product(a, b):
    return dot3(*split(a), *split(b))


def beyond(value, limit):
    rows = value.shape[0] // 8
    over = jnp.where(jnp.abs(value) <= limit, 0.0, 1.0)
    return jnp.max(over.reshape(rows, 8, value.shape[1]), axis=0)


SMEM = pl.BlockSpec(memory_space=pltpu.SMEM)
VMEM = pl.BlockSpec(memory_space=pltpu.VMEM)
ANY = pl.BlockSpec(memory_space=pl.ANY)


def room(mib):
    return pltpu.CompilerParams(vmem_limit_bytes=mib << 20)


def local_kernel(
    pos, d_in, s_in, b_in, ph, pl_, c_out, g0, g1, g2, g3, bad_ref,
    d, s, b, sh, sl, turned, sem,
):
    copies = []
    for j in range(4):
        part = pl.ds(j * 4, 4)
        copies.append(
            [
                pltpu.make_async_copy(source.at[0, part], target.at[part], sem.at[k, j])
                for k, (source, target) in enumerate(((d_in, d), (s_in, s), (b_in, b)))
            ]
        )
        for copy in copies[-1]:
            copy.start()

    def step_of(i):
        if i % 4 == 0:
            for copy in copies[i // 4]:
                copy.wait()
        return -dot(d[i], s[i]), dot(d[i], b[i])

    bad = jnp.zeros((8, B), F32)
    step, own = step_of(0)
    moved = step
    for i in range(KS):
        if i > 0:
            fresh = dot3(*split(step), sh[...], sl[...])
            moved, own = fresh[:, :B], fresh[:, B:] + own
        if i + 1 < KS:
            step, own_next = step_of(i + 1)
        mh, ml = split(moved)
        ph[i], pl_[i], c_out[i] = mh, ml, own
        bad = jnp.maximum(bad, beyond(moved, LIMIT))
        if i + 1 < KS:
            xh, xl = split(own)
            sh[:, :B], sl[:, :B] = mh, ml
            sh[:, B:], sl[:, B:] = xh, xl
            own = own_next
    bad_ref[...] = bad
    moved = moved.T
    turned[...] = own.T
    for step, g in enumerate((g0, g1, g2, g3)):
        g[:B] = moved
        start = pl.multiple_of(lax.rem(pos[0] + step, 4) * Q, Q)
        g[B:] = turned[pl.ds(start, Q), :]


def local_scan(pos, inverse, lower, right):
    piece = jax.ShapeDtypeStruct((B + Q, B), F32)
    return pl.pallas_call(
        local_kernel,
        in_specs=[SMEM] + [ANY] * 3,
        out_specs=[VMEM] * 8,
        out_shape=[
            jax.ShapeDtypeStruct((KS, B, B), BF16),
            jax.ShapeDtypeStruct((KS, B, B), BF16),
            jax.ShapeDtypeStruct((KS, B, B), F32),
            piece, piece, piece, piece,
            jax.ShapeDtypeStruct((8, B), F32),
        ],
        scratch_shapes=[pltpu.VMEM((KS, B, B), BF16)] * 3
        + [pltpu.VMEM((B, 2 * B), BF16)] * 2
        + [pltpu.VMEM((B, B), F32), pltpu.SemaphoreType.DMA((3, 4))],
        compiler_params=room(24),
        name="local_scan",
    )(pos, inverse, lower, right)


def group_kernel(pos, g0, g1, g2, g3, w_ref, wg_ref, bad_ref, buf, sem):
    copies = []
    for step, g in enumerate((g0, g1, g2, g3)):
        place = lax.rem(pos[0] + 4 - step, 4)
        copies.append(pltpu.make_async_copy(g, buf.at[place], sem.at[step]))
    for copy in copies:
        copy.start()
    for copy in copies:
        copy.wait()
    w = buf[0]
    w_ref[0] = w
    bad = jnp.zeros((8, B), F32)
    for k in range(1, 4):
        w = product(w, buf[k, :B])
        w = jnp.concatenate([w[:B], w[B:] + buf[k, B:]], axis=0)
        bad = jnp.maximum(bad, beyond(w[:B], LIMIT))
        if k < 3:
            w_ref[k] = w
    wg_ref[...] = w
    bad_ref[...] = bad


def group_scan(pos, pieces):
    return pl.pallas_call(
        group_kernel,
        in_specs=[SMEM] + [ANY] * 4,
        out_specs=[VMEM] * 3,
        out_shape=[
            jax.ShapeDtypeStruct((3, B + Q, B), F32),
            jax.ShapeDtypeStruct((B + Q, B), F32),
            jax.ShapeDtypeStruct((8, B), F32),
        ],
        scratch_shapes=[pltpu.VMEM((4, B + Q, B), F32), pltpu.SemaphoreType.DMA((4,))],
        compiler_params=room(8),
        name="group_scan",
    )(pos, *pieces)


def pair_kernel(own, other, mh_ref, ml_ref, c_ref, bad_ref):
    z = product(other[...], own[:B])
    bad_ref[...] = beyond(z[:B], LIMIT)
    mh_ref[...], ml_ref[...] = split(z[:B])
    c_ref[...] = z[B:] + own[B:]


def pair_scan(own, other):
    return pl.pallas_call(
        pair_kernel,
        in_specs=[VMEM] * 2,
        out_specs=[VMEM] * 4,
        out_shape=[
            jax.ShapeDtypeStruct((B, B), BF16),
            jax.ShapeDtypeStruct((B, B), BF16),
            jax.ShapeDtypeStruct((Q, B), F32),
            jax.ShapeDtypeStruct((8, B), F32),
        ],
        compiler_params=room(4),
        name="pair_scan",
    )(own, other)


def hop_kernel(x, mh, ml, c, out):
    out[...] = dot3(*split(x[...]), mh[...], ml[...]) + c[...]


def hop(x, mh, ml, c):
    return pl.pallas_call(
        hop_kernel,
        in_specs=[VMEM] * 4,
        out_specs=VMEM,
        out_shape=jax.ShapeDtypeStruct((Q, B), F32),
        compiler_params=room(2),
        name="hop",
    )(x, mh, ml, c)


def start_kernel(pos, z_in, x_in, other, w_ref, o0, o1, o2, o3, all_):
    through = product(z_in[...], other[:B]) + other[B:]
    begin = jnp.where(pos[1] == 1, through, x_in[...])
    all_[0] = begin
    bh, bl = split(begin)
    for k in range(3):
        all_[k + 1] = dot3(bh, bl, *split(w_ref[k, :B])) + w_ref[k, B:]
    for step, o in enumerate((o0, o1, o2, o3)):
        o[...] = all_[lax.rem(pos[0] + step, 4)]


def starts(pos, z_in, x_in, other, w):
    return pl.pallas_call(
        start_kernel,
        in_specs=[SMEM] + [VMEM] * 4,
        out_specs=[VMEM] * 4,
        out_shape=[jax.ShapeDtypeStruct((Q, B), F32)] * 4,
        scratch_shapes=[pltpu.VMEM((4, Q, B), F32)],
        compiler_params=room(5),
        name="starts",
    )(pos, z_in, x_in, other, w)


HALF = 128


def couple(col, tgt, r, xw, acc):
    def four(j, carry):
        for u in range(4):
            k = j * 4 + u
            both = dot(r[0, k], xw[col[k]])
            acc[tgt[k]] += both[:, :HALF] + both[:, HALF:]
        return carry

    lax.fori_loop(0, NT // 4, four, 0)


def expand_kernel(
    pos, col, tgt, q0, q1, q2, q3, bad1, bad2, bad3, ph, pl_, c, r_in,
    sol, keep, acc,
    x, send, xt, xh, xl, sem_out,
):
    def write(i):
        return pltpu.make_async_copy(x.at[i], sol.at[0, i], sem_out.at[i])

    for step, q in enumerate((q0, q1, q2, q3)):
        start = pl.multiple_of(lax.rem(pos[0] + 4 - step, 4) * Q, Q)
        xt[pl.ds(start, Q), :] = q[...]
    xh[...], xl[...] = split(xt[...].T)
    bad = jnp.maximum(jnp.maximum(bad1[...], bad2[...]), bad3[...])
    first = pos[2] == 0

    def four(j, bad):
        for u in range(4):
            i = j * 4 + u
            value = dot3(ph[i], pl_[i], xh[...], xl[...]) + c[i]
            x[i] = value
            write(i).start()
            bad = jnp.maximum(bad, beyond(value, LARGE))
            left, right = value[:, :HALF], value[:, HALF:]
            kh, kl = split(jnp.where(first, left, right))
            keep[i, :, :HALF], keep[i, :, HALF:] = kh, kl
            kh, kl = split(jnp.where(first, right, left))
            send[i, :, :HALF], send[i, :, HALF:] = kh, kl
        return bad

    bad = lax.fori_loop(0, KS // 4, four, bad)
    poison = jnp.where(jnp.max(bad) > 0.0, jnp.nan, 0.0)
    acc[...] = jnp.full(acc.shape, poison, F32)
    couple(col, tgt, r_in, send, acc)

    def done(i, carry):
        write(i).wait()
        return carry

    lax.fori_loop(0, KS, done, 0)


def expand(pos, col, tgt, quarters, ph, pl_, c, bads, root_blocks):
    return pl.pallas_call(
        expand_kernel,
        in_specs=[SMEM] * 3 + [VMEM] * 11,
        out_specs=[ANY, VMEM, VMEM],
        out_shape=[
            jax.ShapeDtypeStruct((1, KS, B, B), F32),
            jax.ShapeDtypeStruct((KS, B, B), BF16),
            jax.ShapeDtypeStruct((ROOTS, B, HALF), F32),
        ],
        scratch_shapes=[
            pltpu.VMEM((KS, B, B), F32),
            pltpu.VMEM((KS, B, B), BF16),
            pltpu.VMEM((B, B), F32),
            pltpu.VMEM((B, B), BF16),
            pltpu.VMEM((B, B), BF16),
            pltpu.SemaphoreType.DMA((KS,)),
        ],
        compiler_params=room(32),
        cost_estimate=pl.CostEstimate(flops=10**10, bytes_accessed=30 << 20, transcendentals=0),
        name="expand",
    )(pos, col, tgt, *quarters, *bads, ph, pl_, c, root_blocks)


def keep_kernel(col, tgt, weights, r, acc):
    acc[...] = jnp.zeros_like(acc)
    couple(col, tgt, r, weights, acc)


def keep_half(col, tgt, weights, root_blocks):
    return pl.pallas_call(
        keep_kernel,
        in_specs=[SMEM] * 2 + [VMEM] * 2,
        out_specs=VMEM,
        out_shape=jax.ShapeDtypeStruct((ROOTS, B, HALF), F32),
        compiler_params=room(14),
        cost_estimate=pl.CostEstimate(flops=5 * 10**9, bytes_accessed=16 << 20, transcendentals=0),
        name="keep_half",
    )(col, tgt, weights, root_blocks)


def chunk(count):
    return jax.ShapeDtypeStruct((count, HALF, HALF), F32)


def first_kernel(pos, kept, came, *outs):
    def one(j, carry):
        for step in range(4):
            y, z = lax.rem(pos[0] + step, 4), lax.rem(pos[3] + step, 4)
            top = z * 8 + j
            outs[step][j] = kept[top, :HALF] + came[top, :HALF]
            low = j * 4 + y
            outs[4 + step][j] = kept[low, HALF:] + came[low, HALF:]
        return carry

    lax.fori_loop(0, 8, one, 0)


def first_sums(pos, kept, came):
    return pl.pallas_call(
        first_kernel,
        in_specs=[SMEM] + [VMEM] * 2,
        out_specs=[VMEM] * 8,
        out_shape=[chunk(8)] * 8,
        compiler_params=room(14),
        name="first_sums",
    )(pos, kept, came)


def second_kernel(pos, *refs):
    ins, outs, held = refs[:8], refs[8:16], refs[16]
    for color in range(2):
        a, b, c, d = (ins[color * 4 + k][...] for k in range(4))
        held[color] = (a + b) + (c + d)
    for step in range(4):
        y, z = lax.rem(pos[0] + step, 4), lax.rem(pos[3] + step, 4)
        for x_hi in range(2):
            outs[step][x_hi] = held[0, x_hi * 4 + y]
            outs[4 + step][x_hi] = held[1, z * 2 + x_hi]


def second_sums(pos, upper, lower):
    return pl.pallas_call(
        second_kernel,
        in_specs=[SMEM] + [VMEM] * 8,
        out_specs=[VMEM] * 8,
        out_shape=[chunk(2)] * 8,
        scratch_shapes=[pltpu.VMEM((2, 8, HALF, HALF), F32)],
        compiler_params=room(12),
        name="second_sums",
    )(pos, *upper, *lower)


def third_kernel(pos, *refs):
    ins, outs, held = refs[:8], refs[8:12], refs[12]
    for color in range(2):
        rows = slice(color * HALF, (color + 1) * HALF)
        a, b, c, d = (ins[color * 4 + k][...] for k in range(4))
        held[:, rows, :] = (a + b) + (c + d)
    for step, out in enumerate(outs):
        out[...] = held[lax.rem(pos[4] + step, 4) // 2]


def third_sums(pos, upper, lower):
    return pl.pallas_call(
        third_kernel,
        in_specs=[SMEM] + [VMEM] * 8,
        out_specs=[VMEM] * 4,
        out_shape=[jax.ShapeDtypeStruct((B, HALF), F32)] * 4,
        scratch_shapes=[pltpu.VMEM((2, B, HALF), F32)],
        compiler_params=room(4),
        name="third_sums",
    )(pos, *upper, *lower)


def last_kernel(a, b, c, d, out):
    out[...] = (a[...] + b[...]) + (c[...] + d[...])


def last_sums(parts):
    return pl.pallas_call(
        last_kernel,
        in_specs=[VMEM] * 4,
        out_specs=VMEM,
        out_shape=jax.ShapeDtypeStruct((B, HALF), F32),
        compiler_params=room(2),
        name="last_sums",
    )(*parts)


def root_kernel(pos, rhs, inv, mine, theirs, out, again):
    first = pos[2] == 0
    left = jnp.where(first, mine[...], theirs[...])
    right = jnp.where(first, theirs[...], mine[...])
    total = jnp.concatenate([left, right], axis=1)
    corner = total[:8, :]
    again[0] = jnp.max(jnp.where(corner != corner, 1.0, 0.0)).astype(jnp.int32)
    uh, ul = split(rhs[0].astype(F32) - total)
    i = inv[0]
    out[0] = dot(jnp.concatenate([i, i], axis=1), jnp.concatenate([uh, ul], axis=0))


def root_solve(pos, rhs, inv, mine, theirs):
    return pl.pallas_call(
        root_kernel,
        in_specs=[SMEM] + [VMEM] * 4,
        out_specs=[VMEM, SMEM],
        out_shape=[
            jax.ShapeDtypeStruct((1, B, B), F32),
            jax.ShapeDtypeStruct((1,), jnp.int32),
        ],
        compiler_params=room(4),
        name="root_solve",
    )(pos, rhs, inv, mine, theirs)


def other_core(value):
    return permute(value, lambda l, c, z, h, y: (l, 1 - c, z, h, y))


def along_x(step):
    def target(l, k, z, h, y):
        x = (h * 2 + l + step) % 4
        return (x % 2, k, z, x // 2, y)

    return target


def along_y(step):
    return lambda l, k, z, h, y: (l, k, z, h, (y + step) % 4)


def along_z(step):
    return lambda l, k, z, h, y: (l, k, (z + step) % 4, h, y)


def exchange(parts, along):
    return [parts[0]] + [permute(parts[step], along(step)) for step in (1, 2, 3)]


def reduce_roots(pos, sent, kept):
    parts = first_sums(pos, kept, other_core(sent))
    parts = second_sums(pos, exchange(parts[:4], along_z), exchange(parts[4:], along_y))
    parts = third_sums(pos, exchange(parts[:4], along_y), exchange(parts[4:], along_z))
    mine = last_sums(exchange(parts, along_x))
    return mine, other_core(mine)


def chain_fast(pos, inverse, lower, right):
    ph, pl_, c, *pieces, bad1 = local_scan(pos, inverse, lower, right)

    pieces = exchange(pieces, along_y)
    w, own, bad2 = group_scan(pos, pieces)
    other = permute(own, lambda l, k, z, h, y: (l, k, z, 1, y) if h == 0 else None)
    mh, ml, cz, bad3 = pair_scan(own, other)

    def up(l, k, z, h, y):
        return (l, k, z + 1, 1, y) if h == 1 and z < 3 else None

    def across(l, k, z, h, y):
        return (l, k, z + 1, 0, y) if h == 1 and z < 3 else None

    x = cz
    x = hop(permute(x, up), mh, ml, cz)
    x = hop(permute(x, up), mh, ml, cz)
    z_in, x_in = permute(x, up), permute(x, across)
    quarters = starts(pos, z_in, x_in, other, w)
    quarters = exchange(quarters, along_y)
    return ph, pl_, c, quarters, (bad1, bad2, bad3)


def sweep_blocks(previous, inverse, lower_blocks, right_side):
    def advance(carry, operands):
        inverse_block, lower_block, right_block = operands
        update = right_block.astype(F32) - jnp.dot(
            lower_block.astype(F32), carry, precision=HIGHEST, preferred_element_type=F32
        )
        solved = jnp.dot(
            inverse_block.astype(F32), update, precision=HIGHEST, preferred_element_type=F32
        )
        return (solved, solved)

    return lax.scan(advance, previous, (inverse, lower_blocks, right_side))


def chain_slow(inverse, lower, right):
    inverse, lower, right = inverse[0], lower[0], right[0]
    position = lax.axis_index("chain")
    length = lax.axis_size("chain")

    def one_turn(turn, carry):
        incoming, solved = carry

        def work(operands):
            return sweep_blocks(operands[0], inverse, lower, right)

        outgoing, solved = lax.cond(turn == position, work, lambda o: o, (incoming, solved))
        incoming = permute(
            outgoing,
            lambda l, k, z, h, y: (
                (l, k, *_place(z * 8 + h * 4 + y + 1)) if z * 8 + h * 4 + y < 31 else None
            ),
        )
        return (incoming, solved)

    begin = (jnp.zeros((B, B), F32), jnp.zeros((KS, B, B), F32))
    return lax.fori_loop(0, length, one_turn, begin)[1]


def _place(index):
    return index // 8, index // 4 % 2, index % 4


def slow_partial(solved, columns, targets, root_blocks):
    def add(partial, operands):
        block, column, target = operands
        term = jnp.dot(
            block.astype(F32), solved[column], precision=HIGHEST, preferred_element_type=F32
        )
        return (partial.at[target].add(term), None)

    zero = jnp.zeros((ROOTS, B, B), F32)
    return lax.scan(add, zero, (root_blocks[0], columns, targets))[0]


def per_device(
    chain_rhs,
    diag_inverse,
    sub_blocks,
    root_blocks,
    coupling_column,
    coupling_target,
    root_rhs,
    root_inverse,
):
    place = lax.axis_index("chain")
    group = lax.axis_index("grp")
    core, x = group % 2, place // 4 % 2 * 2 + group // 2
    pos = jnp.stack([place % 4, place // 4 % 2, core, place // 8, x]).astype(jnp.int32)
    col, tgt = coupling_column[0], coupling_target[0]

    ph, pl_, c, quarters, bads = chain_fast(pos, diag_inverse, sub_blocks, chain_rhs)
    solution_, weights, sent = expand(
        pos, col, tgt, quarters, ph, pl_, c, bads, root_blocks
    )
    kept = keep_half(col, tgt, weights, root_blocks)
    mine, theirs = reduce_roots(pos, sent, kept)
    root, again = root_solve(pos, root_rhs, root_inverse, mine, theirs)

    def redo(state):
        solved = chain_slow(diag_inverse, sub_blocks, chain_rhs)
        partial = slow_partial(solved, col, tgt, root_blocks)
        left, right = partial[:, :, :HALF], partial[:, :, HALF:]
        kept = jnp.where(core == 0, left, right)
        sent = jnp.where(core == 0, right, left)
        mine, theirs = reduce_roots(pos, sent, kept)
        root, _ = root_solve(pos, root_rhs, root_inverse, mine, theirs)
        return (jnp.zeros((1,), jnp.int32), solved[None], root)

    _, solution_, root = lax.while_loop(lambda s: s[0][0] > 0, redo, (again, solution_, root))
    return (solution_, root)


def solution(mesh):
    in_specs = (
        P("grp", "chain", None, None),
        P("grp", "chain", None, None),
        P("grp", "chain", None, None),
        P("grp", "chain", None, None),
        P("grp", "chain"),
        P("grp", "chain"),
        P("chain", None, None),
        P("chain", None, None),
    )
    out_specs = (P("grp", "chain", None, None), P("chain", None, None))
    return jax.shard_map(
        per_device, mesh=mesh, in_specs=in_specs, out_specs=out_specs, check_vma=False
    )
```

```python
import jax
import jax.numpy as jnp
from jax import lax
from jax.experimental import pallas as pl
from jax.experimental.pallas import tpu as pltpu
from jax.sharding import PartitionSpec as P


HIGHEST = lax.Precision.HIGHEST
F32, BF16 = jnp.float32, jnp.bfloat16

B = 256
KS = 16
NT = 32
ROOTS = 32
Q = 64
LIMIT = 16.0
LARGE = 1e28
AXES = ("grp", "chain")


def flat(x_lo, core, z, x_hi, y):
    return (x_lo * 2 + core) * 32 + z * 8 + x_hi * 4 + y


EVERY = [
    (x_lo, core, z, x_hi, y)
    for x_lo in range(2)
    for core in range(2)
    for z in range(4)
    for x_hi in range(2)
    for y in range(4)
]


def permute(value, target):
    pairs = []
    for place in EVERY:
        to = target(*place)
        if to is not None:
            pairs.append((flat(*place), flat(*to)))
    return lax.ppermute(value, AXES, pairs)


def split(value):
    high = value.astype(BF16)
    return high, (value - high.astype(F32)).astype(BF16)


def dot(a, b):
    return jnp.dot(a, b, preferred_element_type=F32)


def dot3(ah, al, bh, bl):
    return dot(
        jnp.concatenate([ah, al, ah], axis=1), jnp.concatenate([bh, bh, bl], axis=0)
    )


def product(a, b):
    return dot3(*split(a), *split(b))


def beyond(value, limit):
    rows = value.shape[0] // 8
    over = jnp.where(jnp.abs(value) <= limit, 0.0, 1.0)
    return jnp.max(over.reshape(rows, 8, value.shape[1]), axis=0)


SMEM = pl.BlockSpec(memory_space=pltpu.SMEM)
VMEM = pl.BlockSpec(memory_space=pltpu.VMEM)
ANY = pl.BlockSpec(memory_space=pl.ANY)


def room(mib):
    return pltpu.CompilerParams(vmem_limit_bytes=mib << 20)


def local_kernel(
    pos, d_in, s_in, b_in, ph, pl_, c_out, g0, g1, g2, g3, bad_ref,
    d, s, b, sh, sl, turned, sem,
):
    copies = []
    for j in range(4):
        part = pl.ds(j * 4, 4)
        copies.append(
            [
                pltpu.make_async_copy(source.at[0, part], target.at[part], sem.at[k, j])
                for k, (source, target) in enumerate(((d_in, d), (s_in, s), (b_in, b)))
            ]
        )
        for copy in copies[-1]:
            copy.start()

    def step_of(i):
        if i % 4 == 0:
            for copy in copies[i // 4]:
                copy.wait()
        return -dot(d[i], s[i]), dot(d[i], b[i])

    bad = jnp.zeros((8, B), F32)
    step, own = step_of(0)
    moved = step
    for i in range(KS):
        if i > 0:
            fresh = dot3(*split(step), sh[...], sl[...])
            moved, own = fresh[:, :B], fresh[:, B:] + own
        if i + 1 < KS:
            step, own_next = step_of(i + 1)
        mh, ml = split(moved)
        ph[i], pl_[i], c_out[i] = mh, ml, own
        bad = jnp.maximum(bad, beyond(moved, LIMIT))
        if i + 1 < KS:
            xh, xl = split(own)
            sh[:, :B], sl[:, :B] = mh, ml
            sh[:, B:], sl[:, B:] = xh, xl
            own = own_next
    bad_ref[...] = bad
    moved = moved.T
    turned[...] = own.T
    for step, g in enumerate((g0, g1, g2, g3)):
        g[:B] = moved
        start = pl.multiple_of(lax.rem(pos[0] + step, 4) * Q, Q)
        g[B:] = turned[pl.ds(start, Q), :]


def local_scan(pos, inverse, lower, right):
    piece = jax.ShapeDtypeStruct((B + Q, B), F32)
    return pl.pallas_call(
        local_kernel,
        in_specs=[SMEM] + [ANY] * 3,
        out_specs=[VMEM] * 8,
        out_shape=[
            jax.ShapeDtypeStruct((KS, B, B), BF16),
            jax.ShapeDtypeStruct((KS, B, B), BF16),
            jax.ShapeDtypeStruct((KS, B, B), F32),
            piece, piece, piece, piece,
            jax.ShapeDtypeStruct((8, B), F32),
        ],
        scratch_shapes=[pltpu.VMEM((KS, B, B), BF16)] * 3
        + [pltpu.VMEM((B, 2 * B), BF16)] * 2
        + [pltpu.VMEM((B, B), F32), pltpu.SemaphoreType.DMA((3, 4))],
        compiler_params=room(24),
        name="local_scan",
    )(pos, inverse, lower, right)


def group_kernel(pos, g0, g1, g2, g3, w_ref, m_ref, c_ref, bad_ref, buf, sem):
    copies = []
    for step, g in enumerate((g0, g1, g2, g3)):
        place = lax.rem(pos[0] + 4 - step, 4)
        copies.append(pltpu.make_async_copy(g, buf.at[place], sem.at[step]))
    for copy in copies:
        copy.start()
    for copy in copies:
        copy.wait()
    w = buf[0]
    w_ref[0] = w
    bad = jnp.zeros((8, B), F32)
    for k in range(1, 4):
        w = product(w, buf[k, :B])
        w = jnp.concatenate([w[:B], w[B:] + buf[k, B:]], axis=0)
        bad = jnp.maximum(bad, beyond(w[:B], LIMIT))
        if k < 3:
            w_ref[k] = w
    m_ref[...], c_ref[...] = w[:B], w[B:]
    bad_ref[...] = bad


def group_scan(pos, pieces):
    return pl.pallas_call(
        group_kernel,
        in_specs=[SMEM] + [ANY] * 4,
        out_specs=[VMEM] * 4,
        out_shape=[
            jax.ShapeDtypeStruct((3, B + Q, B), F32),
            jax.ShapeDtypeStruct((B, B), F32),
            jax.ShapeDtypeStruct((Q, B), F32),
            jax.ShapeDtypeStruct((8, B), F32),
        ],
        scratch_shapes=[pltpu.VMEM((4, B + Q, B), F32), pltpu.SemaphoreType.DMA((4,))],
        compiler_params=room(8),
        name="group_scan",
    )(pos, *pieces)


def pair_kernel(own, other, mh_ref, ml_ref, bad_ref):
    z = product(other[...], own[...])
    bad_ref[...] = beyond(z, LIMIT)
    mh_ref[...], ml_ref[...] = split(z)


def pair_scan(own, other):
    return pl.pallas_call(
        pair_kernel,
        in_specs=[VMEM] * 2,
        out_specs=[VMEM] * 3,
        out_shape=[
            jax.ShapeDtypeStruct((B, B), BF16),
            jax.ShapeDtypeStruct((B, B), BF16),
            jax.ShapeDtypeStruct((8, B), F32),
        ],
        compiler_params=room(4),
        name="pair_scan",
    )(own, other)


def carry_kernel(x, m, c, out):
    out[...] = product(x[...], m[...]) + c[...]


def carry_on(x, m, c):
    return pl.pallas_call(
        carry_kernel,
        in_specs=[VMEM] * 3,
        out_specs=VMEM,
        out_shape=jax.ShapeDtypeStruct((Q, B), F32),
        compiler_params=room(2),
        name="carry_on",
    )(x, m, c)


def hop_kernel(x, mh, ml, c, out):
    out[...] = dot3(*split(x[...]), mh[...], ml[...]) + c[...]


def hop(x, mh, ml, c):
    return pl.pallas_call(
        hop_kernel,
        in_specs=[VMEM] * 4,
        out_specs=VMEM,
        out_shape=jax.ShapeDtypeStruct((Q, B), F32),
        compiler_params=room(2),
        name="hop",
    )(x, mh, ml, c)


def start_kernel(pos, z_in, x_in, m, c, w_ref, o0, o1, o2, o3, all_):
    through = product(z_in[...], m[...]) + c[...]
    begin = jnp.where(pos[1] == 1, through, x_in[...])
    all_[0] = begin
    bh, bl = split(begin)
    for k in range(3):
        all_[k + 1] = dot3(bh, bl, *split(w_ref[k, :B])) + w_ref[k, B:]
    for step, o in enumerate((o0, o1, o2, o3)):
        o[...] = all_[lax.rem(pos[0] + step, 4)]


def starts(pos, z_in, x_in, m, c, w):
    return pl.pallas_call(
        start_kernel,
        in_specs=[SMEM] + [VMEM] * 5,
        out_specs=[VMEM] * 4,
        out_shape=[jax.ShapeDtypeStruct((Q, B), F32)] * 4,
        scratch_shapes=[pltpu.VMEM((4, Q, B), F32)],
        compiler_params=room(5),
        name="starts",
    )(pos, z_in, x_in, m, c, w)


HALF = 128


def couple(col, tgt, r, xw, acc):
    def four(j, carry):
        for u in range(4):
            k = j * 4 + u
            both = dot(r[0, k], xw[col[k]])
            acc[tgt[k]] += both[:, :HALF] + both[:, HALF:]
        return carry

    lax.fori_loop(0, NT // 4, four, 0)


def expand_kernel(
    pos, col, tgt, q0, q1, q2, q3, bad1, bad2, bad3, ph, pl_, c, r,
    value, kh_ref, kl_ref, acc,
    send, xt, xh, xl,
):
    for step, q in enumerate((q0, q1, q2, q3)):
        start = pl.multiple_of(lax.rem(pos[0] + 4 - step, 4) * Q, Q)
        xt[pl.ds(start, Q), :] = q[...]
    core = pos[2]
    keep = pl.ds(pl.multiple_of(core * HALF, HALF), HALF)
    away = pl.ds(pl.multiple_of((1 - core) * HALF, HALF), HALF)
    xh[...], xl[...] = split(xt[away, :].T)
    kh_ref[...], kl_ref[...] = split(xt[keep, :].T)
    bad = jnp.maximum(jnp.maximum(bad1[...], bad2[...]), bad3[...])
    bad = jnp.maximum(bad, beyond(xt[...], LARGE))

    def four(j, bad):
        for u in range(4):
            i = j * 4 + u
            part = c[i, :, away]
            x = dot3(ph[i], pl_[i], xh[...], xl[...]) + part
            value[i] = x
            over = jnp.maximum(beyond(x, LARGE), beyond(c[i, :, keep], LARGE))
            bad = jnp.maximum(bad, jnp.concatenate([over, over], axis=1))
            send[i, :, :HALF], send[i, :, HALF:] = split(x)
        return bad

    bad = lax.fori_loop(0, KS // 4, four, bad)
    poison = jnp.where(jnp.max(bad) > 0.0, jnp.nan, 0.0)
    acc[...] = jnp.full(acc.shape, poison, F32)
    couple(col, tgt, r, send, acc)


def expand(pos, col, tgt, quarters, ph, pl_, c, bads, root_blocks):
    return pl.pallas_call(
        expand_kernel,
        in_specs=[SMEM] * 3 + [VMEM] * 11,
        out_specs=[VMEM] * 4,
        out_shape=[
            jax.ShapeDtypeStruct((KS, B, HALF), F32),
            jax.ShapeDtypeStruct((B, HALF), BF16),
            jax.ShapeDtypeStruct((B, HALF), BF16),
            jax.ShapeDtypeStruct((ROOTS, B, HALF), F32),
        ],
        scratch_shapes=[
            pltpu.VMEM((KS, B, B), BF16),
            pltpu.VMEM((B, B), F32),
            pltpu.VMEM((B, HALF), BF16),
            pltpu.VMEM((B, HALF), BF16),
        ],
        compiler_params=room(26),
        cost_estimate=pl.CostEstimate(flops=10**10, bytes_accessed=30 << 20, transcendentals=0),
        name="expand",
    )(pos, col, tgt, *quarters, *bads, ph, pl_, c, root_blocks)


def keep_kernel(
    pos, col, tgt, value, kh, kl, ph, pl_, c, r, sol, acc, x, weights, sem
):
    core = pos[2]
    keep = pl.ds(pl.multiple_of(core * HALF, HALF), HALF)
    away = pl.ds(pl.multiple_of((1 - core) * HALF, HALF), HALF)

    def write(i):
        return pltpu.make_async_copy(x.at[i], sol.at[0, i], sem.at[i])

    def four(j, carry):
        for u in range(4):
            i = j * 4 + u
            mine = dot3(ph[i], pl_[i], kh[...], kl[...]) + c[i, :, keep]
            x[i, :, keep] = mine
            x[i, :, away] = value[i]
            weights[i, :, :HALF], weights[i, :, HALF:] = split(mine)
            write(i).start()
        return carry

    lax.fori_loop(0, KS // 4, four, 0)
    acc[...] = jnp.zeros_like(acc)
    couple(col, tgt, r, weights, acc)

    def done(i, carry):
        write(i).wait()
        return carry

    lax.fori_loop(0, KS, done, 0)


def keep_half(pos, col, tgt, value, kh, kl, ph, pl_, c, root_blocks):
    return pl.pallas_call(
        keep_kernel,
        in_specs=[SMEM] * 3 + [VMEM] * 7,
        out_specs=[ANY, VMEM],
        out_shape=[
            jax.ShapeDtypeStruct((1, KS, B, B), F32),
            jax.ShapeDtypeStruct((ROOTS, B, HALF), F32),
        ],
        scratch_shapes=[
            pltpu.VMEM((KS, B, B), F32),
            pltpu.VMEM((KS, B, B), BF16),
            pltpu.SemaphoreType.DMA((KS,)),
        ],
        compiler_params=room(30),
        cost_estimate=pl.CostEstimate(flops=5 * 10**9, bytes_accessed=16 << 20, transcendentals=0),
        name="keep_half",
    )(pos, col, tgt, value, kh, kl, ph, pl_, c, root_blocks)


def chunk(count):
    return jax.ShapeDtypeStruct((count, HALF, HALF), F32)


def first_kernel(pos, kept, came, *outs):
    def one(j, carry):
        for step in range(4):
            y, z = lax.rem(pos[0] + step, 4), lax.rem(pos[3] + step, 4)
            top = z * 8 + j
            outs[step][j] = kept[top, :HALF] + came[top, :HALF]
            low = j * 4 + y
            outs[4 + step][j] = kept[low, HALF:] + came[low, HALF:]
        return carry

    lax.fori_loop(0, 8, one, 0)


def first_sums(pos, kept, came):
    return pl.pallas_call(
        first_kernel,
        in_specs=[SMEM] + [VMEM] * 2,
        out_specs=[VMEM] * 8,
        out_shape=[chunk(8)] * 8,
        compiler_params=room(14),
        name="first_sums",
    )(pos, kept, came)


def second_kernel(pos, *refs):
    ins, outs, held = refs[:8], refs[8:16], refs[16]
    for color in range(2):
        a, b, c, d = (ins[color * 4 + k][...] for k in range(4))
        held[color] = (a + b) + (c + d)
    for step in range(4):
        y, z = lax.rem(pos[0] + step, 4), lax.rem(pos[3] + step, 4)
        for x_hi in range(2):
            outs[step][x_hi] = held[0, x_hi * 4 + y]
            outs[4 + step][x_hi] = held[1, z * 2 + x_hi]


def second_sums(pos, upper, lower):
    return pl.pallas_call(
        second_kernel,
        in_specs=[SMEM] + [VMEM] * 8,
        out_specs=[VMEM] * 8,
        out_shape=[chunk(2)] * 8,
        scratch_shapes=[pltpu.VMEM((2, 8, HALF, HALF), F32)],
        compiler_params=room(12),
        name="second_sums",
    )(pos, *upper, *lower)


def third_kernel(pos, *refs):
    ins, outs, held = refs[:8], refs[8:12], refs[12]
    for color in range(2):
        rows = slice(color * HALF, (color + 1) * HALF)
        a, b, c, d = (ins[color * 4 + k][...] for k in range(4))
        held[:, rows, :] = (a + b) + (c + d)
    for step, out in enumerate(outs):
        out[...] = held[lax.rem(pos[4] + step, 4) // 2]


def third_sums(pos, upper, lower):
    return pl.pallas_call(
        third_kernel,
        in_specs=[SMEM] + [VMEM] * 8,
        out_specs=[VMEM] * 4,
        out_shape=[jax.ShapeDtypeStruct((B, HALF), F32)] * 4,
        scratch_shapes=[pltpu.VMEM((2, B, HALF), F32)],
        compiler_params=room(4),
        name="third_sums",
    )(pos, *upper, *lower)


def last_kernel(a, b, c, d, out):
    out[...] = (a[...] + b[...]) + (c[...] + d[...])


def last_sums(parts):
    return pl.pallas_call(
        last_kernel,
        in_specs=[VMEM] * 4,
        out_specs=VMEM,
        out_shape=jax.ShapeDtypeStruct((B, HALF), F32),
        compiler_params=room(2),
        name="last_sums",
    )(*parts)


def root_kernel(pos, rhs, inv, mine, theirs, out, again):
    first = pos[2] == 0
    left = jnp.where(first, mine[...], theirs[...])
    right = jnp.where(first, theirs[...], mine[...])
    total = jnp.concatenate([left, right], axis=1)
    corner = total[:8, :]
    again[0] = jnp.max(jnp.where(corner != corner, 1.0, 0.0)).astype(jnp.int32)
    uh, ul = split(rhs[0].astype(F32) - total)
    i = inv[0]
    out[0] = dot(jnp.concatenate([i, i], axis=1), jnp.concatenate([uh, ul], axis=0))


def root_solve(pos, rhs, inv, mine, theirs):
    return pl.pallas_call(
        root_kernel,
        in_specs=[SMEM] + [VMEM] * 4,
        out_specs=[VMEM, SMEM],
        out_shape=[
            jax.ShapeDtypeStruct((1, B, B), F32),
            jax.ShapeDtypeStruct((1,), jnp.int32),
        ],
        compiler_params=room(4),
        name="root_solve",
    )(pos, rhs, inv, mine, theirs)


def other_core(value):
    return permute(value, lambda l, c, z, h, y: (l, 1 - c, z, h, y))


def along_x(step):
    def target(l, k, z, h, y):
        x = (h * 2 + l + step) % 4
        return (x % 2, k, z, x // 2, y)

    return target


def along_y(step):
    return lambda l, k, z, h, y: (l, k, z, h, (y + step) % 4)


def along_z(step):
    return lambda l, k, z, h, y: (l, k, (z + step) % 4, h, y)


def exchange(parts, along):
    return [parts[0]] + [permute(parts[step], along(step)) for step in (1, 2, 3)]


def reduce_roots(pos, sent, kept):
    parts = first_sums(pos, kept, other_core(sent))
    parts = second_sums(pos, exchange(parts[:4], along_z), exchange(parts[4:], along_y))
    parts = third_sums(pos, exchange(parts[:4], along_y), exchange(parts[4:], along_z))
    mine = last_sums(exchange(parts, along_x))
    return mine, other_core(mine)


def chain_fast(pos, inverse, lower, right):
    ph, pl_, c, *pieces, bad1 = local_scan(pos, inverse, lower, right)

    pieces = exchange(pieces, along_y)
    w, m_own, c_own, bad2 = group_scan(pos, pieces)

    def pair(l, k, z, h, y):
        return (l, k, z, 1, y) if h == 0 else None

    c_other = permute(c_own, pair)
    m_other = permute(m_own, pair)
    cz = carry_on(c_other, m_own, c_own)

    def up(l, k, z, h, y):
        return (l, k, z + 1, 1, y) if h == 1 and z < 3 else None

    def across(l, k, z, h, y):
        return (l, k, z + 1, 0, y) if h == 1 and z < 3 else None

    x = permute(cz, up)
    mh, ml, bad3 = pair_scan(m_own, m_other)
    x = hop(x, mh, ml, cz)
    x = hop(permute(x, up), mh, ml, cz)
    z_in, x_in = permute(x, up), permute(x, across)
    quarters = starts(pos, z_in, x_in, m_other, c_other, w)
    quarters = exchange(quarters, along_y)
    return ph, pl_, c, quarters, (bad1, bad2, bad3)


def sweep_blocks(previous, inverse, lower_blocks, right_side):
    def advance(carry, operands):
        inverse_block, lower_block, right_block = operands
        update = right_block.astype(F32) - jnp.dot(
            lower_block.astype(F32), carry, precision=HIGHEST, preferred_element_type=F32
        )
        solved = jnp.dot(
            inverse_block.astype(F32), update, precision=HIGHEST, preferred_element_type=F32
        )
        return (solved, solved)

    return lax.scan(advance, previous, (inverse, lower_blocks, right_side))


def chain_slow(inverse, lower, right):
    inverse, lower, right = inverse[0], lower[0], right[0]
    position = lax.axis_index("chain")
    length = lax.axis_size("chain")

    def one_turn(turn, carry):
        incoming, solved = carry

        def work(operands):
            return sweep_blocks(operands[0], inverse, lower, right)

        outgoing, solved = lax.cond(turn == position, work, lambda o: o, (incoming, solved))
        incoming = permute(
            outgoing,
            lambda l, k, z, h, y: (
                (l, k, *_place(z * 8 + h * 4 + y + 1)) if z * 8 + h * 4 + y < 31 else None
            ),
        )
        return (incoming, solved)

    begin = (jnp.zeros((B, B), F32), jnp.zeros((KS, B, B), F32))
    return lax.fori_loop(0, length, one_turn, begin)[1]


def _place(index):
    return index // 8, index // 4 % 2, index % 4


def slow_partial(solved, columns, targets, root_blocks):
    def add(partial, operands):
        block, column, target = operands
        term = jnp.dot(
            block.astype(F32), solved[column], precision=HIGHEST, preferred_element_type=F32
        )
        return (partial.at[target].add(term), None)

    zero = jnp.zeros((ROOTS, B, B), F32)
    return lax.scan(add, zero, (root_blocks[0], columns, targets))[0]


def per_device(
    chain_rhs,
    diag_inverse,
    sub_blocks,
    root_blocks,
    coupling_column,
    coupling_target,
    root_rhs,
    root_inverse,
):
    place = lax.axis_index("chain")
    group = lax.axis_index("grp")
    core, x = group % 2, place // 4 % 2 * 2 + group // 2
    pos = jnp.stack([place % 4, place // 4 % 2, core, place // 8, x]).astype(jnp.int32)
    col, tgt = coupling_column[0], coupling_target[0]

    ph, pl_, c, quarters, bads = chain_fast(pos, diag_inverse, sub_blocks, chain_rhs)
    value, kh, kl, sent = expand(
        pos, col, tgt, quarters, ph, pl_, c, bads, root_blocks
    )
    solution_, kept = keep_half(
        pos, col, tgt, value, kh, kl, ph, pl_, c, root_blocks
    )
    mine, theirs = reduce_roots(pos, sent, kept)
    root, again = root_solve(pos, root_rhs, root_inverse, mine, theirs)

    def redo(state):
        solved = chain_slow(diag_inverse, sub_blocks, chain_rhs)
        partial = slow_partial(solved, col, tgt, root_blocks)
        left, right = partial[:, :, :HALF], partial[:, :, HALF:]
        kept = jnp.where(core == 0, left, right)
        sent = jnp.where(core == 0, right, left)
        mine, theirs = reduce_roots(pos, sent, kept)
        root, _ = root_solve(pos, root_rhs, root_inverse, mine, theirs)
        return (jnp.zeros((1,), jnp.int32), solved[None], root)

    _, solution_, root = lax.while_loop(lambda s: s[0][0] > 0, redo, (again, solution_, root))
    return (solution_, root)


def solution(mesh):
    in_specs = (
        P("grp", "chain", None, None),
        P("grp", "chain", None, None),
        P("grp", "chain", None, None),
        P("grp", "chain", None, None),
        P("grp", "chain"),
        P("grp", "chain"),
        P("chain", None, None),
        P("chain", None, None),
    )
    out_specs = (P("grp", "chain", None, None), P("chain", None, None))
    return jax.shard_map(
        per_device, mesh=mesh, in_specs=in_specs, out_specs=out_specs, check_vma=False
    )
```
